32 devices in a mesh: bulk: 4 (over y, x), wide: 8 (over z, core).
Axes of the slice: x: 2, y: 2, z: 4, core: 2. Of those that a mesh axis runs over, the one named last changes fastest.
Arguments:
- particle_cell: int32 [32, 512], P(('bulk', 'wide')), may hold values from 0 to 4095
- particle_frac: float32 [32, 512], P(('bulk', 'wide')), may hold values from 0 to 1
- particle_mass: float32 [32, 512], P(('bulk', 'wide')), may hold values from 0.5 to 2
- particle_vel: float32 [3, 32, 512], P(None, ('bulk', 'wide')), may hold values from -6 to 6
- node_cell: int32 [256, 256], P(('bulk', 'wide')), may hold values from 0 to 4095
- node_body: int32 [256, 256], P(('bulk', 'wide')), may hold values from 0 to 511
- node_count: int32 [256], P(('bulk', 'wide')), may hold values from 1 to 256, as said below
- node_pos: float32 [3, 256, 256], P(None, ('bulk', 'wide')), may hold values from -4 to 4
- body_state: float32 [12, 16384], P(None, ('bulk', 'wide')), may hold values from -4 to 4, as said below
- body_vel: float32 [12, 16384], P(None, ('bulk', 'wide')), may hold values from -3 to 3
- body_mass: float32 [16384], P(('bulk', 'wide')), may hold values from 1 to 4
- touch_body: int32 [256, 128], P(('bulk', 'wide')), may hold values from 0 to 511
- touch_pos: float32 [3, 256, 128], P(None, ('bulk', 'wide')), may hold values from -4 to 4
Outputs:
- body_next: float32 [12, 16384], P(None, ('bulk', 'wide'))
- grid_velocity: float32 [3, 64, 8, 256], P(None, 'bulk', 'wide')
- touch_point: float32 [3, 256, 128], P(None, ('bulk', 'wide'))
The draws below stay inside these ranges and needn't reach their ends.
Inputs may be any that keep to these rules, and one draw needn't show every extreme that they name: `node_count`: for each device and owner, the live node slots; every draw has an owner that receives 256 live rows from every device. `body_state`: rows 3 to 11 hold a 3 x 3 matrix within 0.3 of the identity in every entry; rows 0 to 2 within -4 to 4. `touch_body`: every device lists 128 touch slots for every owner.
All inputs are finite; a program needn't handle non-finite values.
Results may differ from the reference program's by a relative error of at most 0.0018.
Values sent between devices are 32-bit elements; how exact they have to be, the bound alone decides.
A program may use at most 64 MiB of HBM per device.

```python
import math
import jax
import jax.numpy as jnp
from jax import lax

LAYERS = 16
COLUMNS = 256
BR = 1
PPB = 512
BOD_DEV = 512
CAP = 256
TCAP = 128
BODIES = 16384
N_BULK = 4
N_WIDE = 8
DEVICES = 32


def draw_node_count(key, part):
    first_key, second_key, third_key = jax.random.split(jax.random.fold_in(key, 11), 3)
    first = jax.random.randint(first_key, (DEVICES * N_WIDE,), 1, CAP + 1)
    second = jax.random.randint(second_key, (DEVICES * N_WIDE,), 1, CAP + 1)
    counts = jnp.minimum(first, second)
    busiest = jax.random.randint(third_key, (), 0, N_WIDE)
    owners = jnp.arange(DEVICES * N_WIDE, dtype=jnp.int32) % N_WIDE
    return jnp.where(owners == busiest, CAP, counts).astype(jnp.int32)


def draw_body_state(key, part):
    first_key, second_key = jax.random.split(jax.random.fold_in(key, 23), 2)
    shifts = jnp.clip(1.5 * jax.random.normal(first_key, (3, BODIES), jnp.float32), -4.0, 4.0)
    noise = jnp.clip(0.15 * jax.random.normal(second_key, (9, BODIES), jnp.float32), -0.3, 0.3)
    identity = jnp.eye(3, dtype=jnp.float32).reshape(9, 1)
    return jnp.concatenate([shifts, identity + noise], axis=0).astype(jnp.float32)


def with_ends(result, rng, least, top_value):
    spot = [jax.random.randint(jax.random.fold_in(rng, axis), (), 0, length) for axis, length in enumerate(result.shape)]
    longest = result.shape.index(max(result.shape))
    neighbour = spot[:longest] + [(spot[longest] + 1) % result.shape[longest]] + spot[longest + 1:]
    return result.at[tuple(spot)].set(least).at[tuple(neighbour)].set(top_value)


def block_levels(stream_key, dims, pieces, smallest, largest):
    def one(axis_at, shards_of):
        steps = jax.random.uniform(jax.random.fold_in(jax.random.fold_in(stream_key, 6), axis_at), (shards_of,), jnp.float32, smallest / len(pieces), largest / len(pieces))
        return jnp.repeat(jnp.exp(steps), dims[axis_at] // shards_of).reshape((-1,) + (1,) * (len(dims) - axis_at - 1))

    level = one(*pieces[0])
    for cut in pieces[1:]:
        level = level * one(*cut)
    return level


def bell_draw(key, extent, spread, most, pieces=(), held_as=jnp.bfloat16):
    values = jax.random.normal(key, extent, jnp.float32) * spread
    if len(pieces) > 0:
        values = block_levels(key, extent, pieces, -0.22, 0.18) * values
    return jnp.clip(values, min=-most, max=most).astype(held_as)


def setup_inputs(seed: int = 0) -> dict:
    arg_keys = jax.random.split(jax.random.key(seed), 14)
    return {
        "particle_cell": with_ends(jax.random.randint(arg_keys[0], (DEVICES * BR, PPB), 0, LAYERS * COLUMNS), jax.random.fold_in(arg_keys[0], 1), 0, (LAYERS * COLUMNS) - 1).astype(jnp.int32),
        "particle_frac": jnp.clip(1.0 * jax.random.uniform(arg_keys[1], (DEVICES * BR, PPB), jnp.float32) ** block_levels(arg_keys[1], (DEVICES * BR, PPB), ((0, 32),), -0.2, 0.2), 0.0, 1.0),
        "particle_mass": jnp.clip(jnp.exp(math.log(2.0) - 1.3862944 * jax.random.uniform(arg_keys[2], (DEVICES * BR, PPB), jnp.float32) ** block_levels(arg_keys[2], (DEVICES * BR, PPB), ((0, 32),), -0.2, 0.2)), 0.5, 2.0),
        "particle_vel": bell_draw(arg_keys[3], (3, DEVICES * BR, PPB), 1.0, 6.0, ((1, 32),), jnp.float32),
        "node_cell": with_ends(jax.random.randint(arg_keys[4], (DEVICES * N_WIDE, CAP), 0, LAYERS * BR * COLUMNS), jax.random.fold_in(arg_keys[4], 1), 0, (LAYERS * BR * COLUMNS) - 1).astype(jnp.int32),
        "node_body": with_ends(jax.random.randint(arg_keys[5], (DEVICES * N_WIDE, CAP), 0, BOD_DEV), jax.random.fold_in(arg_keys[5], 1), 0, BOD_DEV - 1).astype(jnp.int32),
        "node_count": draw_node_count(jax.random.fold_in(arg_keys[13], 71), 0),
        "node_pos": bell_draw(arg_keys[7], (3, DEVICES * N_WIDE, CAP), 1.0, 4.0, ((1, 32),), jnp.float32),
        "body_state": draw_body_state(jax.random.fold_in(arg_keys[13], 71), 0),
        "body_vel": bell_draw(arg_keys[9], (12, BODIES), 0.5, 3.0, ((1, 32),), jnp.float32),
        "body_mass": jnp.clip(jnp.exp(math.log(4.0) - 1.3862944 * jax.random.uniform(arg_keys[10], (BODIES,), jnp.float32) ** block_levels(arg_keys[10], (BODIES,), ((0, 32),), -0.2, 0.2)), 1.0, 4.0),
        "touch_body": with_ends(jax.random.randint(arg_keys[11], (DEVICES * N_WIDE, TCAP), 0, BOD_DEV), jax.random.fold_in(arg_keys[11], 1), 0, BOD_DEV - 1).astype(jnp.int32),
        "touch_pos": bell_draw(arg_keys[12], (3, DEVICES * N_WIDE, TCAP), 1.0, 4.0, ((1, 32),), jnp.float32),
    }


stiffness = 0.05
gravity_pull = -0.5


def brick_values(cells, fractions, masses, velocities):
    lower = 1.0 - fractions
    upper = fractions
    moments = masses[None] * velocities
    stacked = jnp.concatenate([(masses * lower)[None], moments * lower[None], (masses * upper)[None], moments * upper[None]], axis=0)
    return stacked.astype(jnp.bfloat16)


def extend_brick(totals):
    extended = jnp.zeros((4, (LAYERS + 1) * COLUMNS), jnp.float32)
    extended = extended.at[:, :LAYERS * COLUMNS].add(totals[:4])
    return extended.at[:, COLUMNS:].add(totals[4:])


def brick_sums(operands):
    cells, fractions, masses, velocities = operands
    values = brick_values(cells, fractions, masses, velocities).astype(jnp.float32)
    totals = jnp.zeros((8, LAYERS * COLUMNS), jnp.float32).at[:, cells].add(values)
    return extend_brick(totals)


def solve_nine(matrix, right_hand):
    matrix_rows = [matrix[number] for number in range(9)]
    right_side = [right_hand[number] for number in range(9)]
    for column in range(9):
        for lower_row in range(column + 1, 9):
            factor = matrix_rows[lower_row][column] / matrix_rows[column][column]
            matrix_rows[lower_row] = matrix_rows[lower_row] - factor * matrix_rows[column]
            right_side[lower_row] = right_side[lower_row] - factor * right_side[column]
    answer = [None] * 9
    for column in reversed(range(9)):
        residual = right_side[column]
        for column_after in range(column + 1, 9):
            residual = residual - matrix_rows[column][column_after] * answer[column_after]
        answer[column] = residual / matrix_rows[column][column]
    return jnp.stack(answer)


def newton_step(states, velocities, masses, forces):
    highest = lax.Precision.HIGHEST
    batch_size = states.shape[1]
    identity = jnp.eye(3, dtype=jnp.float32)
    affine = states[3:].reshape(3, 3, batch_size)
    moved = states[:3] + velocities[:3] + forces[:3] / masses[None]
    strain = jnp.einsum("imb,jmb->ijb", affine, affine, precision=highest) - identity[:, :, None]
    restoring = 4.0 * jnp.einsum("imb,mjb->ijb", strain, affine, precision=highest)
    gram = jnp.einsum("mlb,mjb->ljb", affine, affine, precision=highest)
    first = identity[:, None, :, None, None] * gram[None, :, None, :, :]
    second = jnp.einsum("ilb,kjb->ijklb", affine, affine, precision=highest)
    third = strain[:, None, :, None, :] * identity[None, :, None, :, None]
    hessian = (4.0 * stiffness) * (first + second + third).reshape(9, 9, batch_size)
    hessian = hessian + masses[None, None] * jnp.eye(9, dtype=jnp.float32)[:, :, None]
    right_hand = masses[None] * velocities[3:] + forces[3:] - stiffness * restoring.reshape(9, batch_size)
    update = solve_nine(hessian, right_hand)
    return jnp.concatenate([moved, states[3:] + update], axis=0)


def place_points(picked, positions):
    affine = picked[3:].reshape((3, 3) + picked.shape[1:])
    return picked[:3] + jnp.einsum("ijst,jst->ist", affine, positions, precision=lax.Precision.HIGHEST)


def reference(particle_cell, particle_frac, particle_mass, particle_vel, node_cell, node_body, node_count, node_pos, body_state, body_vel, body_mass, touch_body, touch_pos):
    bulk_count = N_BULK
    wide_count = N_WIDE
    bricks = lax.map(brick_sums, (particle_cell, particle_frac, particle_mass, jnp.moveaxis(particle_vel, 1, 0)))
    bricks = bricks.reshape(bulk_count, wide_count, BR, 4, LAYERS + 1, COLUMNS)
    interior = bricks[:, :, :, :, :LAYERS]
    ghost_layer = bricks[:, :, :, :, LAYERS]
    interior = interior.at[1:, :, :, :, 0].add(ghost_layer[:-1])
    mass_grid = interior[:, :, :, 0]
    pull_vector = jnp.array([0.0, 0.0, gravity_pull], jnp.float32)
    velocity = interior[:, :, :, 1:] / (mass_grid[:, :, :, None] + 1.0) + pull_vector[None, None, None, :, None, None]
    layer_ids = jnp.arange(bulk_count, dtype=jnp.int32)[:, None] * LAYERS + jnp.arange(LAYERS, dtype=jnp.int32)[None]
    walls = (layer_ids == 0) | (layer_ids == bulk_count * LAYERS - 1)
    velocity = jnp.where(walls[:, None, None, None, :, None], jnp.float32(0.0), velocity)
    grid_velocity = jnp.transpose(velocity, (3, 0, 4, 1, 2, 5)).reshape(3, bulk_count * LAYERS, wide_count * BR, COLUMNS)
    cells_device = LAYERS * BR * COLUMNS
    mass_flat = jnp.transpose(mass_grid, (0, 1, 3, 2, 4)).reshape(bulk_count, wide_count, cells_device)
    velocity_flat = jnp.transpose(velocity, (0, 1, 3, 4, 2, 5)).reshape(bulk_count, wide_count, 3, cells_device)
    node_index = node_cell.reshape(bulk_count, wide_count, wide_count * CAP)
    node_mass = jnp.take_along_axis(mass_flat, node_index, axis=2)
    wide_index = jnp.broadcast_to(node_index[:, :, None], (bulk_count, wide_count, 3, wide_count * CAP))
    node_velocity = jnp.take_along_axis(velocity_flat, wide_index, axis=3)
    push = (node_mass[:, :, None] * node_velocity).reshape(bulk_count, wide_count, 3, wide_count, CAP)
    live = jnp.arange(CAP, dtype=jnp.int32)[None, None, None, :] < node_count.reshape(bulk_count, wide_count, wide_count)[:, :, :, None]
    push = jnp.where(live[:, :, None], push, jnp.float32(0.0))
    offsets = jnp.moveaxis(node_pos.reshape(3, bulk_count, wide_count, wide_count, CAP), 0, 2)
    outer = (push[:, :, :, None] * offsets[:, :, None]).reshape(bulk_count, wide_count, 9, wide_count, CAP)
    general = jnp.concatenate([push, outer], axis=2)
    row_base = (jnp.arange(bulk_count, dtype=jnp.int32)[:, None, None, None] * wide_count + jnp.arange(wide_count, dtype=jnp.int32)[None, None, :, None]) * BOD_DEV
    owners = row_base + node_body.reshape(bulk_count, wide_count, wide_count, CAP)
    forces = jnp.zeros((12, BODIES), jnp.float32).at[:, owners.reshape(-1)].add(jnp.moveaxis(general, 2, 0).reshape(12, -1))
    body_next = newton_step(body_state, body_vel, body_mass, forces)
    touched = row_base + touch_body.reshape(bulk_count, wide_count, wide_count, TCAP)
    picked = body_next[:, touched.reshape(-1)].reshape(12, bulk_count * wide_count * wide_count, TCAP)
    touch_point = place_points(picked, touch_pos)
    return body_next, grid_velocity, touch_point
```

```python
import functools

import jax
import jax.numpy as jnp
from jax import lax
from jax.experimental import pallas as pl
from jax.experimental.pallas import tpu as pltpu
from jax.sharding import PartitionSpec as P

LAYERS = 16
COLUMNS = 256
LANES = 128
MESH = pl.DeviceIdType.MESH

stiffness = 0.05
gravity_pull = -0.5


def split_parts(value):
    coarse = value.astype(jnp.bfloat16).astype(jnp.float32)
    return coarse, value - coarse


def one_hot(ids, rows):
    found = lax.broadcasted_iota(jnp.int32, (rows, ids.shape[1]), 0) == ids
    return jnp.where(found, 1.0, 0.0).astype(jnp.bfloat16)


def dot_nt(left, right):
    return lax.dot_general(
        left, right, (((1,), (1,)), ((), ())), preferred_element_type=jnp.float32
    )


def particle_sums(cells, fractions, masses, velocities):
    particles = cells.shape[1]
    layer, column = cells // COLUMNS, cells % COLUMNS
    below = 1.0 - fractions
    moments = [masses] + [masses * velocities[axis] for axis in range(3)]
    lower = [moment * below for moment in moments]
    upper = [moment * fractions for moment in moments]
    layer_ids = lax.broadcasted_iota(jnp.int32, (LAYERS, particles), 0)
    here, next_up = layer_ids == layer, layer_ids == layer + 1
    rows = [
        jnp.where(here, low, jnp.where(next_up, high, 0.0)) for low, high in zip(lower, upper)
    ]
    channel_ids = lax.broadcasted_iota(jnp.int32, (8, particles), 0)
    past = jnp.zeros((8, particles), jnp.float32)
    for channel in range(4):
        past = jnp.where(channel_ids == channel, upper[channel], past)
    past = jnp.where(layer == LAYERS - 1, past, 0.0)
    table = jnp.concatenate(rows + [past], axis=0).astype(jnp.bfloat16)
    return dot_nt(table, one_hot(column, COLUMNS))


def factorise(affine, masses):
    strain, gram = {}, {}
    for i in range(3):
        for j in range(i, 3):
            strain[i, j] = sum(affine[i][m] * affine[j][m] for m in range(3))
            if i == j:
                strain[i, j] = strain[i, j] - 1.0
            gram[i, j] = sum(affine[m][i] * affine[m][j] for m in range(3))
            strain[j, i], gram[j, i] = strain[i, j], gram[i, j]
    matrix = {}
    for row in range(9):
        i, j = divmod(row, 3)
        for other in range(row, 9):
            k, l = divmod(other, 3)
            entry = affine[i][l] * affine[k][j]
            if i == k:
                entry = entry + gram[l, j]
            if j == l:
                entry = entry + strain[i, k]
            entry = (4.0 * stiffness) * entry
            if row == other:
                entry = entry + masses
            matrix[row, other] = entry
    factors, inverses = {}, []
    for column in range(9):
        inverse = 1.0 / matrix[column, column]
        inverses.append(inverse)
        for row in range(column + 1, 9):
            factors[row, column] = matrix[column, row] * inverse
        for row in range(column + 1, 9):
            for other in range(row, 9):
                matrix[row, other] = (
                    matrix[row, other] - factors[row, column] * matrix[column, other]
                )
    restoring = [
        4.0 * sum(strain[i, m] * affine[m][j] for m in range(3))
        for i in range(3)
        for j in range(3)
    ]
    return factors, inverses, restoring


def kernel(
    bulk_size,
    wide_size,
    cell_ref,
    frac_ref,
    pmass_ref,
    pvel_ref,
    node_cell_ref,
    node_body_ref,
    count_ref,
    node_pos_ref,
    state_ref,
    bvel_ref,
    bmass_ref,
    touch_body_ref,
    touch_pos_ref,
    next_ref,
    grid_ref,
    point_ref,
    ghost_out,
    ghost_in,
    body_in,
    pos_in,
    tbody_in,
    tpos_in,
    push_out,
    push_in,
    point_out,
    point_in,
    states,
    speeds,
    weights,
    solver,
    node_hot,
    body_hot,
    touch_hot,
    send_sem,
    recv_sem,
    ghost_sem,
):
    bulk, wide = lax.axis_index("bulk"), lax.axis_index("wide")
    slots = node_cell_ref.shape[1]
    touches = touch_body_ref.shape[1]
    heads = state_ref.shape[1] // LANES
    pieces = 2 * heads
    following = lax.rem(bulk + 1, bulk_size)
    previous = lax.rem(bulk + bulk_size - 1, bulk_size)
    peers = [lax.rem(wide + step, wide_size) for step in range(1, wide_size)]

    barrier = pltpu.get_barrier_semaphore()
    for peer in peers:
        pl.semaphore_signal(barrier, inc=1, device_id=(bulk, peer), device_id_type=MESH)
    for other in (following, previous):
        pl.semaphore_signal(barrier, inc=1, device_id=(other, wide), device_id_type=MESH)

    sums = particle_sums(
        cell_ref[...], frac_ref[...], pmass_ref[...], [pvel_ref[axis] for axis in range(3)]
    )
    ghost_out[...] = sums[4 * LAYERS :]

    pl.semaphore_wait(barrier, wide_size + 1)

    ghost = pltpu.make_async_remote_copy(
        src_ref=ghost_out,
        dst_ref=ghost_in,
        send_sem=ghost_sem.at[0],
        recv_sem=ghost_sem.at[1],
        device_id=(following, wide),
        device_id_type=MESH,
    )
    ghost.start()

    def exchange(kind, source, target, is_row):
        def pick(ref, index):
            row = pl.ds(index, 1)
            return ref.at[row, :] if is_row else ref.at[:, row, :]

        sends = []
        for number, peer in enumerate(peers):
            sends.append(
                pltpu.make_async_remote_copy(
                    src_ref=pick(source, peer),
                    dst_ref=pick(target, wide),
                    send_sem=send_sem.at[kind, number],
                    recv_sem=recv_sem.at[kind, wide],
                    device_id=(bulk, peer),
                    device_id_type=MESH,
                )
            )
            sends[-1].start()
        if is_row:
            target[pl.ds(wide, 1), :] = source[pl.ds(wide, 1), :]
        else:
            target[:, pl.ds(wide, 1), :] = source[:, pl.ds(wide, 1), :]

        def arrive():
            for number, peer in enumerate(peers):
                pltpu.make_async_remote_copy(
                    src_ref=pick(source, peer),
                    dst_ref=pick(target, peer),
                    send_sem=send_sem.at[kind, number],
                    recv_sem=recv_sem.at[kind, peer],
                    device_id=(bulk, peer),
                    device_id_type=MESH,
                ).wait_recv()

        def leave():
            for send in sends:
                send.wait_send()

        return arrive, leave

    early = [
        exchange(0, node_body_ref, body_in, True),
        exchange(1, touch_body_ref, tbody_in, True),
        exchange(2, node_pos_ref, pos_in, False),
        exchange(3, touch_pos_ref, tpos_in, False),
    ]

    for owner in range(wide_size):
        node_hot[owner] = one_hot(node_cell_ref[owner : owner + 1, :] % COLUMNS, COLUMNS)

    for channel in range(12):
        for head in range(heads):
            lanes = slice(head * LANES, (head + 1) * LANES)
            for copy in range(2):
                place = slice(copy * heads + head, copy * heads + head + 1)
                states[channel, place, :] = state_ref[channel : channel + 1, lanes]
                speeds[channel, place, :] = bvel_ref[channel : channel + 1, lanes]
    for head in range(heads):
        for copy in range(2):
            place = slice(copy * heads + head, copy * heads + head + 1)
            weights[place, :] = bmass_ref[head : head + 1, :]

    ghost.wait()
    layer_ids = lax.broadcasted_iota(jnp.int32, (LAYERS, COLUMNS), 0)
    keep = jnp.logical_and(layer_ids == 0, bulk > 0)
    grid = [
        sums[channel * LAYERS : (channel + 1) * LAYERS]
        + jnp.where(keep, ghost_in[channel : channel + 1, :], 0.0)
        for channel in range(4)
    ]
    whole_ids = layer_ids + bulk * LAYERS
    walls = jnp.logical_or(whole_ids == 0, whole_ids == bulk_size * LAYERS - 1)
    tables = []
    velocities = []
    for axis in range(3):
        velocity = grid[axis + 1] / (grid[0] + 1.0)
        if axis == 2:
            velocity = velocity + gravity_pull
        velocity = jnp.where(walls, 0.0, velocity)
        velocities.append(velocity)
        tables.extend(split_parts(grid[0] * velocity))
    table = jnp.concatenate(tables, axis=0).astype(jnp.bfloat16)

    node_layers = lax.broadcasted_iota(jnp.int32, (LAYERS, slots), 0)
    slot_ids = lax.broadcasted_iota(jnp.int32, (1, slots), 1)
    for owner in range(wide_size):
        found = jnp.dot(table, node_hot[owner], preferred_element_type=jnp.float32)
        chosen = node_layers == node_cell_ref[owner : owner + 1, :] // COLUMNS
        live = slot_ids < count_ref[owner]
        for axis in range(3):
            start = 2 * LAYERS * axis
            both = found[start : start + LAYERS] + found[start + LAYERS : start + 2 * LAYERS]
            push = jnp.sum(jnp.where(chosen, both, 0.0), axis=0, keepdims=True)
            push_out[axis, owner : owner + 1, :] = jnp.where(live, push, 0.0)

    push_arrive, push_leave = exchange(4, push_out, push_in, False)

    for axis in range(3):
        grid_ref[axis] = velocities[axis]

    affine = [[states[3 + 3 * i + j] for j in range(3)] for i in range(3)]
    weight = weights[...]
    factors, inverses, restoring = factorise(affine, weight)
    names = {}
    for name, value in (
        [(key, value) for key, value in factors.items()]
        + [(("inverse", number), value) for number, value in enumerate(inverses)]
        + [
            (("right", number), weight * speeds[3 + number] - stiffness * restoring[number])
            for number in range(9)
        ]
        + [(("moved", number), states[number] + speeds[number]) for number in range(3)]
        + [(("lightness", 0), 1.0 / weight)]
    ):
        names[name] = len(names)
        solver[names[name]] = value

    for arrive, leave in early:
        arrive()
    piece_ids = lax.broadcasted_iota(jnp.int32, (pieces, slots), 0)
    for source in range(wide_size):
        body_hot[source] = one_hot(body_in[source : source + 1, :] % LANES, LANES)
        touch_hot[:, source * touches : (source + 1) * touches] = one_hot(
            tbody_in[source : source + 1, :] % LANES, LANES
        )

    push_arrive()
    force = [push_in[axis] for axis in range(3)]
    arm = [pos_in[axis] for axis in range(3)]
    general = force + [force[i] * arm[j] for i in range(3) for j in range(3)]
    totals = jnp.zeros((12 * pieces, LANES), jnp.float32)
    for source in range(wide_size):
        chosen = piece_ids % heads == body_in[source : source + 1, :] // LANES
        rows = []
        for value in general:
            coarse, rest = split_parts(value[source : source + 1, :])
            rows.append(jnp.where(chosen, jnp.where(piece_ids < heads, coarse, rest), 0.0))
        left = jnp.concatenate(rows, axis=0).astype(jnp.bfloat16)
        totals = totals + dot_nt(left, body_hot[source])

    sums_of = []
    for channel in range(12):
        total = totals[channel * pieces : (channel + 1) * pieces]
        sums_of.append(total + pltpu.roll(total, heads, 0))
    following_state = [
        solver[names["moved", number]] + sums_of[number] * solver[names["lightness", 0]]
        for number in range(3)
    ]
    answer = [solver[names["right", number]] + sums_of[3 + number] for number in range(9)]
    for column in range(9):
        for row in range(column + 1, 9):
            answer[row] = answer[row] - solver[names[row, column]] * answer[column]
    for column in range(9):
        answer[column] = answer[column] * solver[names["inverse", column]]
    for column in reversed(range(9)):
        for row in range(column):
            answer[row] = answer[row] - solver[names[column, row]] * answer[column]
    following_state += [states[3 + number] + answer[number] for number in range(9)]

    first_half = lax.broadcasted_iota(jnp.int32, (pieces, LANES), 0) < heads
    body_table = jnp.concatenate(
        [jnp.where(first_half, *split_parts(value)) for value in following_state], axis=0
    ).astype(jnp.bfloat16)
    looked_up = jnp.dot(body_table, touch_hot[...], preferred_element_type=jnp.float32)
    touch_pieces = lax.broadcasted_iota(jnp.int32, (pieces, touches), 0) % heads
    for source in range(wide_size):
        chosen = touch_pieces == tbody_in[source : source + 1, :] // LANES
        lanes = slice(source * touches, (source + 1) * touches)
        place = [tpos_in[axis, source : source + 1, :] for axis in range(3)]

        def part(channel):
            return looked_up[channel * pieces : (channel + 1) * pieces, lanes]

        for i in range(3):
            point = part(i)
            for j in range(3):
                point = point + part(3 + 3 * i + j) * place[j]
            point_out[i, source : source + 1, :] = jnp.sum(
                jnp.where(chosen, point, 0.0), axis=0, keepdims=True
            )

    point_arrive, point_leave = exchange(5, point_out, point_in, False)

    for channel in range(12):
        for head in range(heads):
            lanes = slice(head * LANES, (head + 1) * LANES)
            next_ref[channel : channel + 1, lanes] = following_state[channel][head : head + 1, :]

    for arrive, leave in early:
        leave()
    push_leave()
    point_leave()
    point_arrive()
    point_ref[...] = point_in[...]


def per_device(
    particle_cell,
    particle_frac,
    particle_mass,
    particle_vel,
    node_cell,
    node_body,
    node_count,
    node_pos,
    body_state,
    body_vel,
    body_mass,
    touch_body,
    touch_pos,
):
    bulk_size, wide_size = lax.axis_size("bulk"), lax.axis_size("wide")
    body_count = body_state.shape[1]
    slots, touches = node_cell.shape[1], touch_body.shape[1]
    pieces = 2 * (body_count // LANES)
    vmem = pl.BlockSpec(memory_space=pltpu.VMEM)
    smem = pl.BlockSpec(memory_space=pltpu.SMEM)
    f32, i32, bf16 = jnp.float32, jnp.int32, jnp.bfloat16
    body_next, velocity, touch_point = pl.pallas_call(
        functools.partial(kernel, bulk_size, wide_size),
        name="substep",
        out_shape=(
            jax.ShapeDtypeStruct(body_state.shape, f32),
            jax.ShapeDtypeStruct((3, LAYERS, COLUMNS), f32),
            jax.ShapeDtypeStruct(touch_pos.shape, f32),
        ),
        in_specs=[vmem] * 6 + [smem] + [vmem] * 6,
        out_specs=(vmem, vmem, vmem),
        scratch_shapes=[
            pltpu.VMEM((8, COLUMNS), f32),
            pltpu.VMEM((8, COLUMNS), f32),
            pltpu.VMEM((wide_size, slots), i32),
            pltpu.VMEM((3, wide_size, slots), f32),
            pltpu.VMEM((wide_size, touches), i32),
            pltpu.VMEM((3, wide_size, touches), f32),
            pltpu.VMEM((3, wide_size, slots), f32),
            pltpu.VMEM((3, wide_size, slots), f32),
            pltpu.VMEM((3, wide_size, touches), f32),
            pltpu.VMEM((3, wide_size, touches), f32),
            pltpu.VMEM((12, pieces, LANES), f32),
            pltpu.VMEM((12, pieces, LANES), f32),
            pltpu.VMEM((pieces, LANES), f32),
            pltpu.VMEM((58, pieces, LANES), f32),
            pltpu.VMEM((wide_size, COLUMNS, slots), bf16),
            pltpu.VMEM((wide_size, LANES, slots), bf16),
            pltpu.VMEM((LANES, wide_size * touches), bf16),
            pltpu.SemaphoreType.DMA((6, wide_size)),
            pltpu.SemaphoreType.DMA((6, wide_size)),
            pltpu.SemaphoreType.DMA((2,)),
        ],
        compiler_params=pltpu.CompilerParams(collective_id=0, has_side_effects=True),
    )(
        particle_cell,
        particle_frac,
        particle_mass,
        particle_vel,
        node_cell,
        node_body,
        node_count,
        node_pos,
        body_state,
        body_vel,
        body_mass.reshape(-1, LANES),
        touch_body,
        touch_pos,
    )
    return body_next, velocity[:, :, None, :], touch_point


def solution(mesh):
    split = ("bulk", "wide")
    placed = (
        P(split, None),
        P(split, None),
        P(split, None),
        P(None, split, None),
        P(split, None),
        P(split, None),
        P(split),
        P(None, split, None),
        P(None, split),
        P(None, split),
        P(split),
        P(split, None),
        P(None, split, None),
    )
    return jax.shard_map(
        per_device,
        mesh=mesh,
        in_specs=placed,
        out_specs=(
            P(None, split),
            P(None, "bulk", "wide", None),
            P(None, split, None),
        ),
        check_vma=False,
    )
```
